32 devices in a mesh: fsdp: 8 (over y, x, core), seq: 4 (over z).
Axes of the slice: x: 2, y: 2, z: 4, core: 2. Of those that a mesh axis runs over, the one named last changes fastest.
Arguments:
- hidden_in: bfloat16 [8, 1024, 2048], P('fsdp', 'seq'), may hold values from -6 to 6
- lengths: int32 [8], P('fsdp'), may hold values from 512 to 1024, as said below
- cotangent: bfloat16 [8, 1024, 2048], P('fsdp', 'seq'), may hold values from -6 to 6
- in_weight: bfloat16 [2048, 6144], P(('fsdp', 'seq')), may hold values from -0.125 to 0.125
- in_bias: bfloat16 [6144], P(('fsdp', 'seq')), may hold values from -0.29882812 to 0.29882812
- out_weight: bfloat16 [2048, 2048], P(('fsdp', 'seq')), may hold values from -1 to 1
- out_bias: bfloat16 [2048], P(('fsdp', 'seq')), may hold values from -2 to 2
- up_weight: bfloat16 [8192, 2048], P(('fsdp', 'seq')), may hold values from -0.125 to 0.125
- up_bias: bfloat16 [8192], P(('fsdp', 'seq')), may hold values from -2 to 2
- down_weight: bfloat16 [8192, 2048], P(('fsdp', 'seq')), may hold values from -0.0625 to 0.0625
- down_bias: bfloat16 [2048], P(('fsdp', 'seq')), may hold values from -2 to 2
- first_gain: bfloat16 [2048], P(('fsdp', 'seq')), may hold values from 0.5 to 1.5
- first_shift: bfloat16 [2048], P(('fsdp', 'seq')), may hold values from -2 to 2
- second_gain: bfloat16 [2048], P(('fsdp', 'seq')), may hold values from 0.5 to 1.5
- second_shift: bfloat16 [2048], P(('fsdp', 'seq')), may hold values from -2 to 2
Outputs:
- layer_output: float32 [8, 1024, 2048], P('fsdp', 'seq')
- input_gradient: float32 [8, 1024, 2048], P('fsdp', 'seq')
- in_weight_gradient: float32 [2048, 6144], P(('fsdp', 'seq'))
- in_bias_gradient: float32 [6144], P(('fsdp', 'seq'))
- out_weight_gradient: float32 [2048, 2048], P(('fsdp', 'seq'))
- out_bias_gradient: float32 [2048], P(('fsdp', 'seq'))
- up_weight_gradient: float32 [8192, 2048], P(('fsdp', 'seq'))
- up_bias_gradient: float32 [8192], P(('fsdp', 'seq'))
- down_weight_gradient: float32 [8192, 2048], P(('fsdp', 'seq'))
- down_bias_gradient: float32 [2048], P(('fsdp', 'seq'))
- first_gain_gradient: float32 [2048], P(('fsdp', 'seq'))
- first_shift_gradient: float32 [2048], P(('fsdp', 'seq'))
- second_gain_gradient: float32 [2048], P(('fsdp', 'seq'))
- second_shift_gradient: float32 [2048], P(('fsdp', 'seq'))
The draws below stay inside these ranges and needn't reach their ends.
Inputs may be any that keep to these rules, and one draw needn't show every extreme that they name: `lengths`: tokens in use at the front of each slot; in every draw one slot is full and one holds 512 tokens.
All inputs are finite; a program needn't handle non-finite values.
Results may differ from the reference program's by a relative error of at most 0.014.
Values may be sent and summed in bfloat16 or wider, within the bound.
No kernel may reach another device: no remote copies, remote signals or barrier semaphores. Data moves between devices by JAX's collectives and lax.ppermute only.
A program may use at most 384 MiB of HBM per device.

```python
import jax
import jax.numpy as jnp
from jax import lax

D = 2048
HEADS = 16
HEAD_DIM = 128
ROT = 32
FF = 8192
SLOT = 1024
SLOTS = 8


def draw_lengths(key, part):
    first_key, second_key = jax.random.split(jax.random.fold_in(key, 11))
    drawn = jax.random.randint(first_key, (SLOTS,), SLOT // 2, SLOT + 1)
    order = jax.random.permutation(second_key, SLOTS)
    drawn = drawn.at[order[0]].set(SLOT)
    drawn = drawn.at[order[1]].set(SLOT // 2)
    return drawn.astype(jnp.int32)


def steps_of(stream_key, shape, cuts, low, high):
    loudness = 1.0
    for axis_at, shards_of in cuts:
        draws = jax.random.uniform(jax.random.fold_in(jax.random.fold_in(stream_key, 6), axis_at), (shards_of,), jnp.float32, low / len(cuts), high / len(cuts))
        loudness = loudness * jnp.repeat(jnp.exp(draws), shape[axis_at] // shards_of).reshape((-1,) + (1,) * (len(shape) - 1 - axis_at))
    return loudness


def noise(own_key, extent, deviation, limit, cuts=(), kind=jnp.bfloat16):
    array = jax.random.normal(own_key, extent, jnp.float32) * deviation
    if len(cuts) > 0:
        array = steps_of(own_key, extent, cuts, -0.22, 0.18) * array
    return jnp.clip(array, min=-limit, max=limit).astype(kind)


def setup_inputs(seed: int = 0) -> dict:
    key_list = jax.random.split(jax.random.key(seed), 16)
    hidden_in = noise(key_list[0], (SLOTS, SLOT, D), 1.0, 6.0, ((0, 8), (1, 4)))
    lengths = draw_lengths(jax.random.fold_in(key_list[15], 71), 0)
    cotangent = noise(key_list[2], (SLOTS, SLOT, D), 1.0, 6.0, ((0, 8), (1, 4)))
    in_weight = noise(key_list[3], (D, 3 * D), D ** -0.5, 0.125, ((0, 32),))
    in_bias = noise(key_list[4], (3 * D,), 0.05, 0.29882812, ((0, 32),))
    out_weight = noise(key_list[5], (D, D), (D * 16 // SLOT) ** -0.5, 1.0, ((0, 32),))
    out_bias = noise(key_list[6], (D,), 0.3, 2.0, ((0, 32),))
    up_weight = noise(key_list[7], (FF, D), D ** -0.5, 0.125, ((0, 32),))
    up_bias = noise(key_list[8], (FF,), 0.3, 2.0, ((0, 32),))
    down_weight = noise(key_list[9], (FF, D), FF ** -0.5, 0.0625, ((0, 32),))
    down_bias = noise(key_list[10], (D,), 0.3, 2.0, ((0, 32),))
    first_gain = jnp.clip(1.0 + 0.1 * jax.random.normal(key_list[11], (D,), jnp.float32), 0.5, 1.5).astype(jnp.bfloat16)
    first_shift = noise(key_list[12], (D,), 0.3, 2.0, ((0, 32),))
    second_gain = jnp.clip(1.0 + 0.1 * jax.random.normal(key_list[13], (D,), jnp.float32), 0.5, 1.5).astype(jnp.bfloat16)
    second_shift = noise(key_list[14], (D,), 0.3, 2.0, ((0, 32),))
    return dict(hidden_in=hidden_in, lengths=lengths, cotangent=cotangent, in_weight=in_weight, in_bias=in_bias, out_weight=out_weight, out_bias=out_bias, up_weight=up_weight, up_bias=up_bias, down_weight=down_weight, down_bias=down_bias, first_gain=first_gain, first_shift=first_shift, second_gain=second_gain, second_shift=second_shift)


@jax.custom_vjp
def low(v):
    return lax.optimization_barrier(v.astype(jnp.bfloat16)).astype(jnp.float32)

@jax.custom_vjp
def low_back(v):
    return v

def low_keep(v):
    return (low(v), None)

def low_pass(kept, grad):
    return (grad,)

def back_keep(v):
    return (v, None)

def back_low(kept, grad):
    return (low(grad),)
low.defvjp(low_keep, low_pass)
low_back.defvjp(back_keep, back_low)
EPSILON = 1e-05
MASKED_SCORE = -1e+30

def layer_norm(values, norm_gain, norm_shift):
    centred = values - lax.optimization_barrier(jnp.mean(values, axis=-1, keepdims=True))
    spread = lax.optimization_barrier(jnp.mean(centred * centred, axis=-1, keepdims=True))
    return centred * lax.rsqrt(spread + EPSILON) * norm_gain + norm_shift

def rotary_tables(positions):
    halves = jnp.arange(ROT // 2, dtype=jnp.float32)
    frequency = 1.0 / 10000.0 ** (halves * 2.0 / ROT)
    angles = positions.astype(jnp.float32)[:, None] * frequency[None, :]
    angles = jnp.concatenate([angles, angles], axis=1)
    return (jnp.cos(angles), jnp.sin(angles))

def rotate(values, cosine_table, sine_table):
    leading = values[..., :ROT]
    middle = ROT // 2
    turned = jnp.concatenate([-leading[..., middle:], leading[..., :middle]], axis=-1)
    leading = leading * cosine_table[:, None, :] + turned * sine_table[:, None, :]
    return jnp.concatenate([leading, values[..., ROT:]], axis=-1)

def attention(query, key_rows, value_rows, keep_mask):
    block_rows = min(512, SLOT)
    block_count = SLOT // block_rows
    columns = jnp.arange(SLOT)
    scale_factor = HEAD_DIM ** (-0.5)

    def one_block(member):
        query_block, first_row = member
        row_index = first_row + jnp.arange(block_rows)
        scores = jnp.einsum('qhd,khd->hqk', query_block, key_rows, precision=lax.Precision.HIGHEST) * scale_factor
        scores = low_back(scores)
        allowed = (columns[None, :] <= row_index[:, None]) & keep_mask[None, :]
        scores = jnp.where(allowed[None], scores, MASKED_SCORE)
        largest = lax.optimization_barrier(jnp.max(scores, axis=-1, keepdims=True))
        weights = jnp.exp(scores - largest)
        probabilities = weights / lax.optimization_barrier(jnp.sum(weights, axis=-1, keepdims=True))
        return jnp.einsum('hqk,khd->qhd', low(probabilities), value_rows, precision=lax.Precision.HIGHEST)
    starts = jnp.arange(block_count, dtype=jnp.int32) * block_rows
    blocks = query.reshape(block_count, block_rows, HEADS, HEAD_DIM)
    mixed = lax.map(jax.checkpoint(one_block), (blocks, starts))
    return mixed.reshape(SLOT, HEADS, HEAD_DIM)

def forward(source, length, params):
    in_weight, in_bias, out_weight, out_bias, up_weight, up_bias, down_weight, down_bias, first_gain, first_shift, second_gain, second_shift = params
    keep_mask = jnp.arange(SLOT) < length
    cosine_table, sine_table = rotary_tables(jnp.arange(SLOT))
    first_in = low(layer_norm(source, first_gain, first_shift))
    joined = low_back(jnp.dot(first_in, in_weight, precision=lax.Precision.HIGHEST) + in_bias)
    joined = joined.reshape(SLOT, 3, HEADS, HEAD_DIM)
    query = low(low_back(rotate(joined[:, 0], cosine_table, sine_table)))
    key_rows = low(low_back(rotate(joined[:, 1], cosine_table, sine_table)))
    value_rows = low(low_back(joined[:, 2]))
    mixed = low(low_back(attention(query, key_rows, value_rows, keep_mask))).reshape(SLOT, D)
    attn_branch = jnp.dot(mixed, out_weight, precision=lax.Precision.HIGHEST) + out_bias
    second_in = low(layer_norm(source, second_gain, second_shift))
    hidden_pre = low_back(lax.dot_general(second_in, up_weight, (((1,), (1,)), ((), ())), precision=lax.Precision.HIGHEST) + up_bias)
    hidden_act = low(jax.nn.gelu(hidden_pre, approximate=False))
    mlp_branch = jnp.dot(hidden_act, down_weight, precision=lax.Precision.HIGHEST) + down_bias
    return jnp.where(keep_mask[:, None], source + attn_branch + mlp_branch, 0.0)

def reference(hidden_in, lengths, cotangent, in_weight, in_bias, out_weight, out_bias, up_weight, up_bias, down_weight, down_bias, first_gain, first_shift, second_gain, second_shift):
    params = tuple((member.astype(jnp.float32) for member in (in_weight, in_bias, out_weight, out_bias, up_weight, up_bias, down_weight, down_bias, first_gain, first_shift, second_gain, second_shift)))
    zeroes = tuple((jnp.zeros(member.shape, jnp.float32) for member in params))

    def one_slot(totals, member):
        source, length, incoming = member
        result, pull_back = jax.vjp(lambda values, weights: forward(values, length, weights), source.astype(jnp.float32), params)
        input_gradient, param_gradients = pull_back(incoming.astype(jnp.float32))
        summed = tuple((before + extra for before, extra in zip(totals, param_gradients)))
        return (summed, (result, input_gradient))
    gradients, (outputs, input_gradients) = lax.scan(one_slot, zeroes, (hidden_in, lengths, cotangent))
    return (outputs, input_gradients) + gradients
```

```python
import functools

import jax
import jax.numpy as jnp
from jax import lax
from jax.experimental import pallas as pl
from jax.experimental.pallas import tpu as pltpu
from jax.sharding import PartitionSpec as P

HEADS = 16
HEAD_DIM = 128
ROT = 32

EPSILON = 1e-05
MASKED_SCORE = -1e30
AXES = ("fsdp", "seq")
F32 = jnp.float32
BF16 = jnp.bfloat16


def dot(left, right, contract, out=F32):
    return lax.dot_general(
        left, right, ((contract[:1], contract[1:]), ((), ())), preferred_element_type=out
    )


def shift_seq(block, step):
    count = lax.axis_size("seq")
    return lax.ppermute(block, "seq", [(i, (i + step) % count) for i in range(count)])


def flip_fsdp(block, mask):
    count = lax.axis_size("fsdp")
    return lax.ppermute(block, "fsdp", [(i, i ^ mask) for i in range(count)])


def cross_first(block):
    return lax.ppermute(block, "fsdp", [(i, i ^ (2 if i & 1 else 4)) for i in range(8)])


def cross_second(block):
    return lax.ppermute(block, "fsdp", [(i, i ^ (4 if i & 1 else 2)) for i in range(8)])


def cross_masks(place):
    odd = (place & 1) == 1
    return jnp.where(odd, 2, 4), jnp.where(odd, 4, 2)


def put(buffer, block, index):
    return lax.dynamic_update_slice_in_dim(buffer, block[None], index, 0)


def pick(blocks, index):
    return lax.dynamic_index_in_dim(blocks, index, 0, keepdims=False)


def gather_fsdp(block):
    count = lax.axis_size("fsdp")
    if count != 8:
        return lax.all_gather(block, "fsdp", axis=0)
    place = lax.axis_index("fsdp")
    first, second = cross_masks(place)
    by_second = cross_second(block)
    by_first = cross_first(block)
    far = cross_first(by_second)
    full = jnp.zeros((8,) + block.shape, block.dtype)
    full = put(full, block, place)
    full = put(full, flip_fsdp(block, 1), place ^ 1)
    full = put(full, by_second, place ^ second)
    full = put(full, flip_fsdp(by_second, 1), place ^ 1 ^ first)
    full = put(full, by_first, place ^ first)
    full = put(full, flip_fsdp(by_first, 1), place ^ 1 ^ second)
    full = put(full, far, place ^ 6)
    full = put(full, flip_fsdp(far, 1), place ^ 7)
    return full


def scatter_fsdp(blocks):
    count = lax.axis_size("fsdp")
    if count != 8:
        return lax.psum_scatter(blocks, "fsdp", scatter_dimension=0, tiled=False).astype(F32)
    place = lax.axis_index("fsdp")
    first, second = cross_masks(place)

    def paired(mask):
        other = flip_fsdp(pick(blocks, place ^ 1 ^ mask).astype(BF16), 1)
        return other.astype(F32)

    from_pair = {mask: paired(mask) for mask in (6, 2, 4, 0)}
    odd = (place & 1) == 1
    pair_first = jnp.where(odd, from_pair[2], from_pair[4])
    pair_second = jnp.where(odd, from_pair[4], from_pair[2])
    far = pick(blocks, place ^ 6).astype(F32) + from_pair[6]
    got_far = cross_first(far.astype(BF16)).astype(F32)
    near_first = pick(blocks, place ^ first).astype(F32) + pair_first
    got_first = cross_first(near_first.astype(BF16)).astype(F32)
    near_second = pick(blocks, place ^ second).astype(F32) + pair_second + got_far
    got_second = cross_second(near_second.astype(BF16)).astype(F32)
    return pick(blocks, place).astype(F32) + from_pair[0] + got_first + got_second


def gather_seq(block):
    count = lax.axis_size("seq")
    place = lax.axis_index("seq")
    full = jnp.zeros((count,) + block.shape, block.dtype)
    full = put(full, block, place)
    moving = block
    for step in range(1, count):
        moving = shift_seq(moving, 1)
        full = put(full, moving, (place - step) % count)
    return full.reshape((count * block.shape[0],) + block.shape[1:])


def scatter_seq(blocks):
    count = lax.axis_size("seq")
    place = lax.axis_index("seq")
    moving = pick(blocks, (place - 1) % count).astype(BF16)
    for step in range(2, count + 1):
        moving = shift_seq(moving, 1).astype(F32) + pick(blocks, (place - step) % count).astype(F32)
        if step < count:
            moving = moving.astype(BF16)
    return moving


def exchange_seq(blocks):
    count = lax.axis_size("seq")
    place = lax.axis_index("seq")
    full = jnp.zeros(blocks.shape, blocks.dtype)
    full = put(full, pick(blocks, place), place)
    for step in range(1, count):
        got = shift_seq(pick(blocks, (place + step) % count), step)
        full = put(full, got, (place - step) % count)
    return full


def gather_small(vector):
    seq_count, fsdp_count = lax.axis_size("seq"), lax.axis_size("fsdp")
    seq_place, fsdp_place = lax.axis_index("seq"), lax.axis_index("fsdp")
    parts = jnp.stack([vector] + [shift_seq(vector, step) for step in range(1, seq_count)])
    parts = parts[(seq_place - jnp.arange(seq_count)) % seq_count]
    parts = jnp.stack([parts] + [flip_fsdp(parts, mask) for mask in range(1, fsdp_count)])
    return parts[fsdp_place ^ jnp.arange(fsdp_count)]


def scatter_small(everywhere, rows):
    seq_count, fsdp_count = lax.axis_size("seq"), lax.axis_size("fsdp")
    seq_place, fsdp_place = lax.axis_index("seq"), lax.axis_index("fsdp")
    by_seq = jnp.moveaxis(everywhere, 1, 0)
    total = pick(by_seq, seq_place)
    for step in range(1, seq_count):
        total = total + shift_seq(pick(by_seq, (seq_place + step) % seq_count), step)
    by_fsdp = jnp.concatenate([total, rows], axis=1)
    result = pick(by_fsdp, fsdp_place)
    for mask in range(1, fsdp_count):
        result = result + flip_fsdp(pick(by_fsdp, fsdp_place ^ mask), mask)
    return result


def rotary_tables(length):
    halves = jnp.arange(ROT // 2, dtype=F32)
    frequency = 1.0 / 10000.0 ** (halves * 2.0 / ROT)
    angles = jnp.arange(length, dtype=jnp.int32).astype(F32)[:, None] * frequency[None, :]
    cosine, sine = jnp.cos(angles), jnp.sin(angles)
    rest = jnp.zeros((length, HEAD_DIM - ROT), F32)
    nothing = jnp.zeros_like(sine)
    return (
        jnp.concatenate([cosine, cosine, rest + 1.0], axis=1),
        jnp.concatenate([-sine, nothing, rest], axis=1),
        jnp.concatenate([nothing, sine, rest], axis=1),
    )


def turn(values, cosine, lower, upper):
    half = ROT // 2
    return (
        values * cosine
        + pltpu.roll(values, HEAD_DIM - half, 1) * lower
        + pltpu.roll(values, half, 1) * upper
    )


def masked_probs(query, key_rows, first_row, used):
    scores = dot(query, key_rows, (1, 1)) * HEAD_DIM ** (-0.5)
    rows = first_row + lax.broadcasted_iota(jnp.int32, scores.shape, 0)
    columns = lax.broadcasted_iota(jnp.int32, scores.shape, 1)
    scores = jnp.where((columns <= rows) & (columns < used), scores, MASKED_SCORE)
    weights = jnp.exp(scores - jnp.max(scores, axis=1, keepdims=True))
    return weights / jnp.sum(weights, axis=1, keepdims=True)


def attend_kernel(rows, used_ref, q_in, k_in, v_in, cosine, lower, upper, q_out, k_out, v_out, mixed):
    length = q_in.shape[0]
    tables = (cosine[...], lower[...], upper[...])
    q_out[...] = turn(q_in[...], *tables).astype(BF16)
    k_out[...] = turn(k_in[...], *tables).astype(BF16)
    v_out[...] = v_in[...].astype(BF16)
    for start in range(0, length, rows):
        stop = start + rows
        probs = masked_probs(q_out[start:stop], k_out[:stop], start, used_ref[0])
        mixed[start:stop] = dot(probs.astype(BF16), v_out[:stop], (1, 0)).astype(BF16)


def attend_back_kernel(
    rows, used_ref, query, key_rows, value_rows, delta, cosine, lower, upper, q_out, k_out, v_out, k_sum, v_sum
):
    length = query.shape[0]
    scale = HEAD_DIM ** (-0.5)
    k_sum[...] = jnp.zeros_like(k_sum)
    v_sum[...] = jnp.zeros_like(v_sum)
    for start in range(0, length, rows):
        stop = start + rows
        block, block_delta = query[start:stop], delta[start:stop]
        probs = masked_probs(block, key_rows[:stop], start, used_ref[0])
        prob_delta = dot(block_delta, value_rows[:stop], (1, 1))
        row_dot = jnp.sum(probs * prob_delta, axis=1, keepdims=True)
        score_delta = (probs * (prob_delta - row_dot)).astype(BF16)
        query_delta = (dot(score_delta, key_rows[:stop], (1, 0)) * scale).astype(BF16).astype(F32)
        q_out[start:stop] = turn(
            query_delta, cosine[start:stop], -lower[start:stop], -upper[start:stop]
        ).astype(BF16)
        k_sum[:stop] += dot(score_delta, block, (0, 0))
        v_sum[:stop] += dot(probs.astype(BF16), block_delta, (0, 0))
    key_delta = (k_sum[...] * scale).astype(BF16).astype(F32)
    k_out[...] = turn(key_delta, cosine[...], -lower[...], -upper[...]).astype(BF16)
    v_out[...] = v_sum[...].astype(BF16)


def head_spec(length, shift):
    return pl.BlockSpec((length, HEAD_DIM), lambda head: (0, head + shift))


def attend(joined, tables, used, heads):
    length = joined.shape[0]
    table = pl.BlockSpec((length, HEAD_DIM), lambda head: (0, 0))
    shape = jax.ShapeDtypeStruct((length, heads * HEAD_DIM), BF16)
    return pl.pallas_call(
        functools.partial(attend_kernel, min(256, length)),
        grid=(heads,),
        in_specs=[pl.BlockSpec(memory_space=pltpu.SMEM)]
        + [head_spec(length, part * heads) for part in range(3)]
        + [table] * 3,
        out_specs=[head_spec(length, 0)] * 4,
        out_shape=[shape] * 4,
        name="attend",
    )(used, joined, joined, joined, *tables)


def attend_back(query, key_rows, value_rows, delta, tables, used, heads):
    length = query.shape[0]
    table = pl.BlockSpec((length, HEAD_DIM), lambda head: (0, 0))
    shape = jax.ShapeDtypeStruct((length, heads * HEAD_DIM), BF16)
    return pl.pallas_call(
        functools.partial(attend_back_kernel, min(256, length)),
        grid=(heads,),
        in_specs=[pl.BlockSpec(memory_space=pltpu.SMEM)] + [head_spec(length, 0)] * 4 + [table] * 3,
        out_specs=[head_spec(length, 0)] * 3,
        out_shape=[shape] * 3,
        scratch_shapes=[pltpu.VMEM((length, HEAD_DIM), F32)] * 2,
        name="attend_back",
    )(used, query, key_rows, value_rows, delta, *tables)


def normed(values):
    centred = values - jnp.mean(values, axis=-1, keepdims=True)
    scale = lax.rsqrt(jnp.mean(centred * centred, axis=-1, keepdims=True) + EPSILON)
    return centred * scale, scale


def gelu_pair(values):
    cumulative = 0.5 * (1.0 + lax.erf(values * 0.5**0.5))
    density = jnp.exp(-0.5 * values * values) * (0.5 / jnp.pi) ** 0.5
    return values * cumulative, cumulative + values * density


def after(value, *earlier):
    return lax.optimization_barrier((value,) + earlier)[0]


def local(
    hidden_in,
    lengths,
    cotangent,
    in_weight,
    in_bias,
    out_weight,
    out_bias,
    up_weight,
    up_bias,
    down_weight,
    down_bias,
    first_gain,
    first_shift,
    second_gain,
    second_shift,
):
    tokens, width = hidden_in.shape[1:]
    fsdp_count, seq_count = lax.axis_size("fsdp"), lax.axis_size("seq")
    fsdp_place, seq_place = lax.axis_index("fsdp"), lax.axis_index("seq")
    length = tokens * seq_count
    heads = HEADS // seq_count
    head_width = heads * HEAD_DIM
    hidden = up_weight.shape[0] * fsdp_count

    own = hidden_in.reshape(tokens, width)
    full = gather_seq(own)
    positions = seq_place * tokens + jnp.arange(tokens, dtype=jnp.int32)
    keep = (positions < lengths[0])[:, None]
    delta_own = jnp.where(keep, cotangent.reshape(tokens, width), jnp.zeros((), BF16))
    delta = gather_seq(after(delta_own, full))

    small = [in_bias, out_bias, down_bias, first_gain, first_shift, second_gain, second_shift]
    sizes = [member.shape[0] for member in small]
    everywhere = gather_small(jnp.concatenate(small + [up_bias]))
    at, whole = 0, []
    for size in sizes:
        whole.append(everywhere[:, :, at : at + size].reshape(-1).astype(F32))
        at += size
    in_offset, out_offset, down_offset, gain_one, shift_one, gain_two, shift_two = whole
    in_offset = lax.dynamic_index_in_dim(
        in_offset.reshape(3, seq_count, head_width), seq_place, 1, keepdims=False
    ).reshape(1, 3 * head_width)
    up_offset = lax.dynamic_index_in_dim(everywhere[:, :, at:], seq_place, 1, keepdims=False)
    up_offset = up_offset.reshape(1, hidden).astype(F32)

    rows = in_weight.shape[0]
    by_heads = in_weight.reshape(rows, 3, seq_count, head_width).transpose(2, 0, 1, 3)
    by_heads = exchange_seq(by_heads.reshape(seq_count, rows, 3 * head_width))
    by_heads = by_heads.reshape(seq_count * rows, 3 * head_width)
    up = gather_fsdp(up_weight).reshape(hidden, width)
    in_matrix = gather_fsdp(after(by_heads, up)).reshape(width, 3 * head_width)
    down = gather_fsdp(after(down_weight, in_matrix)).reshape(hidden, width)
    total = fsdp_count * seq_count
    mine = lax.ppermute(
        out_weight, AXES, [(i, (i % fsdp_count) * seq_count + i // fsdp_count) for i in range(total)]
    )
    out_matrix = gather_fsdp(after(mine, down)).reshape(head_width, width)

    unit, _ = normed(full.astype(F32))
    first_in = (unit * gain_one + shift_one).astype(BF16)
    second_in = (unit * gain_two + shift_two).astype(BF16)
    tables = rotary_tables(length)
    pre = dot(second_in, up, (1, 1)) + up_offset
    act, slope = gelu_pair(pre)
    act = act.astype(BF16)
    joined = dot(first_in, in_matrix, (1, 0)) + in_offset
    query, key_rows, value_rows, mixed = attend(joined, tables, lengths, heads)
    branches = dot(mixed, out_matrix, (1, 0)) + dot(act, down, (1, 0))
    summed = scatter_seq(branches.reshape(seq_count, tokens, width))
    source = own.astype(F32)
    layer_output = jnp.where(keep, source + summed + (out_offset + down_offset), 0.0)

    mixed_delta = dot(delta, out_matrix, (1, 1), BF16)
    pre_delta = (dot(delta, down, (1, 1)) * slope).astype(BF16)
    down_delta = dot(act, delta, (0, 0), BF16)
    down_gradient = scatter_fsdp(down_delta.reshape(fsdp_count, -1, width))
    out_delta = dot(mixed, delta, (0, 0), BF16)
    out_mine = scatter_fsdp(out_delta.reshape(fsdp_count, -1, width))
    query_delta, key_delta, value_delta = attend_back(
        query, key_rows, value_rows, mixed_delta, tables, lengths, heads
    )
    joined_delta = jnp.concatenate([query_delta, key_delta, value_delta], axis=1)
    up_delta = dot(pre_delta, second_in, (0, 0), BF16)
    up_gradient = scatter_fsdp(up_delta.reshape(fsdp_count, -1, width))
    second_delta = dot(pre_delta, up, (1, 0))
    first_delta = dot(joined_delta, in_matrix, (1, 1))
    in_delta = dot(first_in, joined_delta, (0, 0), BF16)
    in_rows = scatter_fsdp(in_delta.reshape(fsdp_count, -1, 3 * head_width))

    unit_delta = first_delta * gain_one + second_delta * gain_two
    unit_delta = scatter_seq(unit_delta.reshape(seq_count, tokens, width))
    own_unit, own_scale = normed(source)
    source_delta = own_scale * (
        unit_delta
        - jnp.mean(unit_delta, axis=-1, keepdims=True)
        - own_unit * jnp.mean(unit_delta * own_unit, axis=-1, keepdims=True)
    )
    input_gradient = delta_own.astype(F32) + source_delta

    out_gradient = lax.ppermute(
        out_mine, AXES, [((i % fsdp_count) * seq_count + i // fsdp_count, i) for i in range(total)]
    )
    in_gradient = exchange_seq(in_rows.astype(BF16).reshape(seq_count, rows, 3 * head_width))
    in_gradient = in_gradient.reshape(seq_count, rows, 3, head_width).transpose(1, 2, 0, 3)
    in_gradient = in_gradient.reshape(rows, -1).astype(F32)

    in_sum = jnp.sum(joined_delta.astype(F32), axis=0).reshape(3, 1, head_width)
    in_sum = lax.dynamic_update_slice_in_dim(
        jnp.zeros((3, seq_count, head_width), F32), in_sum, seq_place, 1
    )
    bias_sum = jnp.sum(delta_own.astype(F32), axis=0)
    sums = [
        in_sum,
        bias_sum,
        jnp.sum(first_delta * unit, axis=0),
        jnp.sum(first_delta, axis=0),
        jnp.sum(second_delta * unit, axis=0),
        jnp.sum(second_delta, axis=0),
    ]
    sums = jnp.concatenate([member.reshape(fsdp_count, seq_count, -1) for member in sums], axis=2)
    up_sum = jnp.sum(pre_delta.astype(F32), axis=0).reshape(fsdp_count, -1)
    small_sums = scatter_small(sums, up_sum)
    at, pieces = 0, []
    for size in (sizes[0],) + (sizes[1],) * 5 + (up_bias.shape[0],):
        pieces.append(small_sums[at : at + size])
        at += size
    in_bias_gradient, bias_gradient, gain_one_g, shift_one_g, gain_two_g, shift_two_g, up_bias_g = pieces
    return (
        layer_output[None],
        input_gradient[None],
        in_gradient,
        in_bias_gradient,
        out_gradient,
        bias_gradient,
        up_gradient,
        up_bias_g,
        down_gradient,
        bias_gradient,
        gain_one_g,
        shift_one_g,
        gain_two_g,
        shift_two_g,
    )


def solution(mesh):
    tokens, matrix, vector = P("fsdp", "seq", None), P(AXES, None), P(AXES)
    return jax.shard_map(
        local,
        mesh=mesh,
        in_specs=(tokens, P("fsdp"), tokens, matrix, vector, matrix, vector, matrix, vector, matrix)
        + (vector,) * 5,
        out_specs=(tokens, tokens, matrix, vector, matrix, vector, matrix, vector, matrix)
        + (vector,) * 5,
        check_vma=False,
    )
```

```python
import functools

import jax
import jax.numpy as jnp
from jax import lax
from jax.experimental import pallas as pl
from jax.experimental.pallas import tpu as pltpu
from jax.sharding import PartitionSpec as P

HEADS = 16
HEAD_DIM = 128
ROT = 32

EPSILON = 1e-05
MASKED_SCORE = -1e30
AXES = ("fsdp", "seq")
F32 = jnp.float32
BF16 = jnp.bfloat16


def dot(left, right, contract, out=F32):
    return lax.dot_general(
        left, right, ((contract[:1], contract[1:]), ((), ())), preferred_element_type=out
    )


def shift_seq(block, step):
    count = lax.axis_size("seq")
    return lax.ppermute(block, "seq", [(i, (i + step) % count) for i in range(count)])


def flip_fsdp(block, mask):
    count = lax.axis_size("fsdp")
    return lax.ppermute(block, "fsdp", [(i, i ^ mask) for i in range(count)])


def cross_first(block):
    return lax.ppermute(block, "fsdp", [(i, i ^ (2 if i & 1 else 4)) for i in range(8)])


def cross_second(block):
    return lax.ppermute(block, "fsdp", [(i, i ^ (4 if i & 1 else 2)) for i in range(8)])


def cross_masks(place):
    odd = (place & 1) == 1
    return jnp.where(odd, 2, 4), jnp.where(odd, 4, 2)


def put(buffer, block, index):
    return lax.dynamic_update_slice_in_dim(buffer, block[None], index, 0)


def pick(blocks, index):
    return lax.dynamic_index_in_dim(blocks, index, 0, keepdims=False)


def together(*values):
    return lax.optimization_barrier(values)


def piece_places():
    place = lax.axis_index("fsdp")
    first, second = cross_masks(place)
    return [place ^ mask for mask in (0, second, first, 6, 1, 1 ^ first, 1 ^ second, 7)]


def flip_all(pieces):
    return [flip_fsdp(piece, 1) for piece in pieces]


def pair_sum(same, given, index):
    rows = same.shape[0] // 4
    span = slice(index * rows, (index + 1) * rows)
    return same[span].astype(F32) + given[span].astype(F32)


def far_share(same, given):
    return pair_sum(same, given, 3).astype(BF16)


def near_shares(same, given, far):
    first = pair_sum(same, given, 2).astype(BF16)
    return first, (pair_sum(same, given, 1) + far.astype(F32)).astype(BF16)


def send_near(first, second):
    return cross_first(first), cross_second(second)


def sum_near(same, given, got_first, got_second):
    return pair_sum(same, given, 0) + got_first.astype(F32) + got_second.astype(F32)


def joined_by(moving, block):
    return (moving.astype(F32) + block.astype(F32)).astype(BF16)


def scatter_whole(blocks):
    count = lax.axis_size("fsdp")
    rows = blocks.reshape((count, -1) + blocks.shape[1:])
    return lax.psum_scatter(rows, "fsdp", scatter_dimension=0, tiled=False).astype(F32)


def exchange_seq(blocks):
    return lax.all_to_all(blocks, "seq", split_axis=0, concat_axis=0, tiled=True)


def flip_seq(block, mask):
    count = lax.axis_size("seq")
    return lax.ppermute(block, "seq", [(i, i ^ mask) for i in range(count)])


def pack_kernel(*refs):
    out = refs[-1]
    for row, ref in enumerate(refs[:-1]):
        out[row : row + 1, : ref.shape[1]] = ref[...].astype(F32)


def small_over(vectors):
    widest = max(vector.shape[0] for vector in vectors)
    packed = pl.pallas_call(
        pack_kernel,
        out_shape=jax.ShapeDtypeStruct((len(vectors), widest), F32),
        name="pack",
    )(*[vector[None] for vector in vectors])
    return [packed] + [shift_seq(packed, step) for step in range(1, lax.axis_size("seq"))]


def small_everywhere(parts):
    seq_count, fsdp_count = lax.axis_size("seq"), lax.axis_size("fsdp")
    seq_place, fsdp_place = lax.axis_index("seq"), lax.axis_index("fsdp")
    parts = jnp.stack(parts)[(seq_place - jnp.arange(seq_count)) % seq_count]
    parts = jnp.stack([parts] + [flip_fsdp(parts, mask) for mask in range(1, fsdp_count)])
    return parts[fsdp_place ^ jnp.arange(fsdp_count)]


def small_exchange(parts, axis):
    return lax.all_to_all(parts, axis, split_axis=0, concat_axis=0, tiled=True)


def rotary_tables(length):
    halves = jnp.arange(ROT // 2, dtype=F32)
    frequency = 1.0 / 10000.0 ** (halves * 2.0 / ROT)
    angles = jnp.arange(length, dtype=jnp.int32).astype(F32)[:, None] * frequency[None, :]
    cosine, sine = jnp.cos(angles), jnp.sin(angles)
    rest = jnp.zeros((length, HEAD_DIM - ROT), F32)
    nothing = jnp.zeros_like(sine)
    return (
        jnp.concatenate([cosine, cosine, rest + 1.0], axis=1),
        jnp.concatenate([-sine, nothing, rest], axis=1),
        jnp.concatenate([nothing, sine, rest], axis=1),
    )


def turn(values, cosine, lower, upper):
    half = ROT // 2
    return (
        values * cosine
        + pltpu.roll(values, HEAD_DIM - half, 1) * lower
        + pltpu.roll(values, half, 1) * upper
    )


def masked_probs(query, key_rows, start, used):
    scores = dot(query, key_rows, (1, 1)) * HEAD_DIM ** (-0.5)
    rows, stop = scores.shape
    diagonal = scores[:, start:]
    causal = lax.broadcasted_iota(jnp.int32, diagonal.shape, 1) <= lax.broadcasted_iota(
        jnp.int32, diagonal.shape, 0
    )
    diagonal = jnp.where(causal, diagonal, MASKED_SCORE)
    scores = jnp.concatenate([scores[:, :start], diagonal], axis=1) if start else diagonal
    columns = lax.broadcasted_iota(jnp.int32, (1, stop), 1)
    scores = jnp.where(columns < used, scores, MASKED_SCORE)
    weights = jnp.exp(scores - jnp.max(scores, axis=1, keepdims=True))
    return weights * (1.0 / jnp.sum(weights, axis=1, keepdims=True))


def attend_kernel(rows, where, q_in, k_in, v_in, cosine, lower, upper, q_out, k_out, v_out, mixed):
    length = q_in.shape[0]
    count = length // rows

    def at(index):
        return pl.ds(pl.multiple_of(lax.rem(where[1] - index + count, count) * rows, rows), rows)

    for index in range(count):
        span = slice(index * rows, (index + 1) * rows)
        tables = (cosine[span], lower[span], upper[span])
        q_out[span] = turn(q_in[at(index)], *tables).astype(BF16)
        k_out[span] = turn(k_in[at(index)], *tables).astype(BF16)
        v_out[span] = v_in[at(index)].astype(BF16)
    for index in range(count):
        start, stop = index * rows, (index + 1) * rows
        probs = masked_probs(q_out[start:stop], k_out[:stop], start, where[0])
        mixed[at(index)] = dot(probs.astype(BF16), v_out[:stop], (1, 0)).astype(BF16)


def attend_back_kernel(
    rows, piece_count, where, query, key_rows, value_rows, cosine, lower, upper, *refs
):
    count = query.shape[0] // rows
    blocks, rights, refs = refs[:count], refs[count : count + piece_count], refs[count + piece_count :]
    out, k_sum, v_sum, buffer, deltas, right, sems, right_sems = refs
    places = [where[2 + index] for index in range(piece_count)]
    moves = copies(blocks, row_targets(buffer, blocks), sems)
    moves += copies(rights, row_targets(right, rights, places), right_sems)
    start_all(moves)
    wait_all(moves)

    @pl.when(pl.program_id(0) == 0)
    def _():
        deltas[...] = dot(buffer[...], right[...], (1, 1)).astype(BF16)

    delta = deltas.at[:, pl.ds(pl.multiple_of(pl.program_id(0) * HEAD_DIM, HEAD_DIM), HEAD_DIM)]
    scale = HEAD_DIM ** (-0.5)

    def at(index):
        return pl.ds(pl.multiple_of(lax.rem(where[1] - index + count, count) * rows, rows), rows)

    k_sum[...] = jnp.zeros_like(k_sum)
    v_sum[...] = jnp.zeros_like(v_sum)
    for index in range(count):
        start, stop = index * rows, (index + 1) * rows
        span = slice(start, stop)
        block, block_delta = query[span], delta[at(index)]
        probs = masked_probs(block, key_rows[:stop], start, where[0])
        prob_delta = dot(block_delta, value_rows[:stop], (1, 1))
        row_dot = jnp.sum(probs * prob_delta, axis=1, keepdims=True)
        score_delta = (probs * (prob_delta - row_dot)).astype(BF16)
        query_delta = (dot(score_delta, key_rows[:stop], (1, 0)) * scale).astype(BF16).astype(F32)
        out[0, at(index)] = turn(query_delta, cosine[span], -lower[span], -upper[span]).astype(BF16)
        k_sum[:stop] += dot(score_delta, block, (0, 0))
        v_sum[:stop] += dot(probs.astype(BF16), block_delta, (0, 0))
    for index in range(count):
        span = slice(index * rows, (index + 1) * rows)
        key_delta = (k_sum[span] * scale).astype(BF16).astype(F32)
        out[1, at(index)] = turn(key_delta, cosine[span], -lower[span], -upper[span]).astype(BF16)
        out[2, at(index)] = v_sum[span].astype(BF16)


ANYWHERE = pl.BlockSpec(memory_space=pl.ANY)


def cost(flops, moved):
    return pl.CostEstimate(flops=2 * flops, bytes_accessed=2 * moved, transcendentals=0)


def head_spec(length, shift):
    return pl.BlockSpec((length, HEAD_DIM), lambda head: (0, head + shift))


def attend(joined, tables, where, heads, tokens):
    length = joined.shape[0]
    table = pl.BlockSpec((length, HEAD_DIM), lambda head: (0, 0))
    shape = jax.ShapeDtypeStruct((length, heads * HEAD_DIM), BF16)
    return pl.pallas_call(
        functools.partial(attend_kernel, tokens),
        grid=(heads,),
        in_specs=[pl.BlockSpec(memory_space=pltpu.SMEM)]
        + [head_spec(length, part * heads) for part in range(3)]
        + [table] * 3,
        out_specs=[head_spec(length, 0)] * 4,
        out_shape=[shape] * 4,
        name="attend",
        cost_estimate=cost(8 * heads * length * length * HEAD_DIM, 10 * length * heads * HEAD_DIM),
    )(where, joined, joined, joined, *tables)


def attend_back(query, key_rows, value_rows, blocks, rights, tables, where, heads):
    length = query.shape[0]
    tokens, width = blocks[0].shape
    table = pl.BlockSpec((length, HEAD_DIM), lambda head: (0, 0))
    return pl.pallas_call(
        functools.partial(attend_back_kernel, tokens, len(rights)),
        grid=(heads,),
        in_specs=[pl.BlockSpec(memory_space=pltpu.SMEM)]
        + [head_spec(length, 0)] * 3
        + [table] * 3
        + [ANYWHERE] * (len(blocks) + len(rights)),
        out_specs=pl.BlockSpec((3, length, HEAD_DIM), lambda head: (0, 0, head)),
        out_shape=jax.ShapeDtypeStruct((3, length, heads * HEAD_DIM), BF16),
        scratch_shapes=[pltpu.VMEM((length, HEAD_DIM), F32)] * 2
        + [
            pltpu.VMEM((length, width), BF16),
            pltpu.VMEM((length, heads * HEAD_DIM), BF16),
            pltpu.VMEM((heads * HEAD_DIM, width), BF16),
            pltpu.SemaphoreType.DMA((len(blocks),)),
            pltpu.SemaphoreType.DMA((len(rights),)),
        ],
        name="attend_back",
        cost_estimate=cost(
            10 * heads * length * length * HEAD_DIM, 14 * length * heads * HEAD_DIM
        ),
    )(where, query, key_rows, value_rows, *tables, *blocks, *rights)


def whole(array):
    return pl.BlockSpec(array.shape, lambda *_: (0,) * array.ndim)


def copies(refs, targets, sems):
    return [
        pltpu.make_async_copy(ref, target, sems.at[index])
        for index, (ref, target) in enumerate(zip(refs, targets))
    ]


def row_targets(buffer, refs, places=None):
    rows = refs[0].shape[0]
    return [
        buffer.at[pl.ds(pl.multiple_of((index if places is None else places[index]) * rows, rows), rows)]
        for index in range(len(refs))
    ]


def start_all(moves):
    @pl.when(pl.program_id(0) == 0)
    def _():
        for move in moves:
            move.start()


def wait_all(moves, step=0):
    @pl.when(pl.program_id(0) == step)
    def _():
        for move in moves:
            move.wait()


def wait_one(moves, shift=0):
    for index, move in enumerate(moves):
        pl.when(pl.program_id(0) == index + shift)(move.wait)


def norm_kernel(block, gain_one, shift_one, gain_two, shift_two, *refs):
    first, second = refs[-2:]
    unit, _ = normed(block[...].astype(F32))
    first[...] = (unit * gain_one[...] + shift_one[...]).astype(BF16)
    second[...] = (unit * gain_two[...] + shift_two[...]).astype(BF16)


def norm_both(block, index, count, scales, earlier):
    tokens, width = block.shape
    shape = jax.ShapeDtypeStruct((count * tokens, width), BF16)
    return pl.pallas_call(
        norm_kernel,
        grid=(4,),
        in_specs=[pl.BlockSpec((tokens // 4, width), lambda step: (step, 0))]
        + [whole(scale) for scale in scales]
        + [ANYWHERE] * len(earlier),
        out_specs=[pl.BlockSpec((tokens // 4, width), lambda step: (4 * index + step, 0))] * 2,
        out_shape=[shape] * 2,
        input_output_aliases={5: 0, 6: 1} if earlier else {},
        name="norm_both",
        cost_estimate=cost(20 * tokens * width, 6 * tokens * width),
    )(block, *scales, *earlier)


def project_kernel(count, places, left, offset, *refs):
    pieces, out, buffer, sems = refs[:count], refs[count], refs[count + 1], refs[count + 2]
    width = out.shape[1]
    parts = buffer.shape[1] // width
    for part in range(parts):
        columns = slice(part * width, (part + 1) * width)
        moves = copies(
            [piece.at[:, columns] for piece in pieces],
            [target.at[:, columns] for target in row_targets(buffer, pieces, places)],
            sems.at[part],
        )
        start_all(moves)
        wait_all(moves, part)
    columns = pl.ds(pl.multiple_of(pl.program_id(0) * width, width), width)
    out[...] = dot(left[...], buffer[:, columns], (1, 0)) + offset[...]


def project(left, pieces, offset, places, parts):
    length, width = left.shape[0], pieces[0].shape[1] // parts
    return pl.pallas_call(
        functools.partial(project_kernel, len(pieces)),
        grid_spec=pltpu.PrefetchScalarGridSpec(
            num_scalar_prefetch=1,
            grid=(parts,),
            in_specs=[whole(left), pl.BlockSpec((1, width), lambda part, _: (0, part))]
            + [ANYWHERE] * len(pieces),
            out_specs=pl.BlockSpec((length, width), lambda part, _: (0, part)),
            scratch_shapes=[
                pltpu.VMEM((left.shape[1], parts * width), BF16),
                pltpu.SemaphoreType.DMA((parts, len(pieces))),
            ],
        ),
        out_shape=jax.ShapeDtypeStruct((length, parts * width), F32),
        name="project",
        cost_estimate=cost(2 * length * left.shape[1] * parts * width, 2 * length * (left.shape[1] + 2 * parts * width)),
    )(places, left, offset, *pieces)


def hidden_kernel(count, places, second, offset, *refs):
    ups = refs[:count]
    act, slope, buffer, sems = refs[count:]
    rows, step = act.shape[1], pl.program_id(0)
    moves = copies(ups, row_targets(buffer, ups), sems)
    start_all(moves)
    wait_one(moves)
    at = pl.ds(pl.multiple_of(step * rows, rows), rows)
    pre = dot(second[...], buffer[at], (1, 1)) + offset[places[step]]
    high, slant = gelu_pair(pre)
    act[...] = high.astype(BF16)
    slope[...] = slant.astype(BF16)


def hidden_forward(second, offset, ups, places):
    length, width = second.shape
    count, rows = len(ups), ups[0].shape[0]
    hidden = count * rows
    return pl.pallas_call(
        functools.partial(hidden_kernel, count),
        grid_spec=pltpu.PrefetchScalarGridSpec(
            num_scalar_prefetch=1,
            grid=(count,),
            in_specs=[whole(second), whole(offset)] + [ANYWHERE] * count,
            out_specs=[pl.BlockSpec((length, rows), lambda step, _: (0, step))] * 2,
            scratch_shapes=[pltpu.VMEM((hidden, width), BF16), pltpu.SemaphoreType.DMA((count,))],
        ),
        out_shape=[jax.ShapeDtypeStruct((length, hidden), BF16)] * 2,
        name="hidden_forward",
        cost_estimate=cost(2 * length * width * hidden, 2 * (length + hidden) * width),
    )(places, second, offset, *ups)


def branch_kernel(count, places, mixed, act, *refs):
    downs, rights, refs = refs[:count], refs[count : 2 * count], refs[2 * count :]
    outs, (buffer, sems, out_matrix, right_sems) = refs[:-4], refs[-4:]
    tokens, columns = outs[0].shape
    right_moves = copies(rights, row_targets(out_matrix, rights, places), right_sems)
    start_all(right_moves)
    wait_all(right_moves)
    for step in range(buffer.shape[1] // columns):
        place = slice(step * columns, (step + 1) * columns)
        moves = copies(
            [down.at[:, place] for down in downs],
            [target.at[:, place] for target in row_targets(buffer, downs)],
            sems.at[step],
        )
        start_all(moves)
        wait_all(moves, step)
    at = pl.ds(pl.multiple_of(pl.program_id(0) * columns, columns), columns)
    for index, out in enumerate(outs):
        span = slice(index * tokens, (index + 1) * tokens)
        total = dot(mixed[span], out_matrix[:, at], (1, 0)) + dot(act[span], buffer[:, at], (1, 0))
        out[...] = total.astype(BF16)


def branch_forward(mixed, rights, act, downs, places, count):
    length, hidden = act.shape
    tokens, width = length // count, downs[0].shape[1]
    columns = min(512, width)
    return pl.pallas_call(
        functools.partial(branch_kernel, len(downs)),
        grid_spec=pltpu.PrefetchScalarGridSpec(
            num_scalar_prefetch=1,
            grid=(width // columns,),
            in_specs=[whole(mixed), whole(act)] + [ANYWHERE] * (2 * len(downs)),
            out_specs=[pl.BlockSpec((tokens, columns), lambda step, _: (0, step))] * count,
            scratch_shapes=[
                pltpu.VMEM((hidden, width), BF16),
                pltpu.SemaphoreType.DMA((width // columns, len(downs))),
                pltpu.VMEM((mixed.shape[1], width), BF16),
                pltpu.SemaphoreType.DMA((len(rights),)),
            ],
        ),
        out_shape=[jax.ShapeDtypeStruct((tokens, width), BF16)] * count,
        name="branch_forward",
        cost_estimate=cost(
            2 * length * width * (hidden + mixed.shape[1]), 2 * (length + width) * hidden
        ),
    )(places, mixed, act, *downs, *rights)


def outer_kernel(count, both, places, left, *refs):
    blocks = refs[:count]
    outs, (buffer, sems) = refs[count:-2], refs[-2:]
    if len(blocks[0].shape) == 3:
        parts, width = blocks[0].shape[0], blocks[0].shape[2]
        moves = copies(
            [blocks[0].at[part] for part in range(parts)],
            [buffer.at[:, part * width : (part + 1) * width] for part in range(parts)],
            sems,
        )
    else:
        moves = copies(blocks, row_targets(buffer, blocks), sems)
    start_all(moves)
    wait_all(moves)
    result = dot(left[...], buffer[...], (0, 0)).astype(BF16)
    if not both:
        outs[0][...] = result
        return
    half = pl.num_programs(0) // 2

    @pl.when(pl.program_id(0) < half)
    def _():
        outs[0][...] = result

    @pl.when(pl.program_id(0) >= half)
    def _():
        outs[1][...] = result


def outer(left, blocks, rows, places, both=False):
    length, steps = left.shape[0], places.shape[0]
    half = steps // 2
    width = blocks[0].size // length if blocks[0].ndim == 3 else blocks[0].shape[1]
    moves = blocks[0].shape[0] if blocks[0].ndim == 3 else len(blocks)
    if both:
        places = jnp.roll(places, -half)
        out_specs = [
            pl.BlockSpec((rows, width), lambda step, _: (jnp.minimum(step, half - 1), 0)),
            pl.BlockSpec((rows, width), lambda step, _: (jnp.maximum(step - half, 0), 0)),
        ]
        out_shape = [jax.ShapeDtypeStruct((half * rows, width), BF16)] * 2
    else:
        out_specs = [pl.BlockSpec((rows, width), lambda step, _: (step, 0))]
        out_shape = [jax.ShapeDtypeStruct((steps * rows, width), BF16)]
    result = pl.pallas_call(
        functools.partial(outer_kernel, len(blocks), both),
        grid_spec=pltpu.PrefetchScalarGridSpec(
            num_scalar_prefetch=1,
            grid=(steps,),
            in_specs=[pl.BlockSpec((length, rows), lambda step, places: (0, places[step]))]
            + [ANYWHERE] * len(blocks),
            out_specs=out_specs,
            scratch_shapes=[
                pltpu.VMEM((length, width), BF16),
                pltpu.SemaphoreType.DMA((moves,)),
            ],
        ),
        out_shape=out_shape,
        name="outer",
        cost_estimate=cost(2 * length * rows * steps * width, 2 * (length + rows * steps) * width),
    )(places, left, *blocks)
    return result if both else result[0]


def hidden_back_kernel(count, block_count, places, slope, *refs):
    downs, blocks = refs[:count], refs[count : count + block_count]
    out, sums, buffer, down_buffer, sems, down_sems = refs[count + block_count :]
    moves = copies(blocks, row_targets(buffer, blocks), sems)
    down_moves = copies(downs, row_targets(down_buffer, downs), down_sems)
    start_all(moves + down_moves)
    wait_all(moves)
    wait_one(down_moves)
    rows, step = out.shape[1], pl.program_id(0)
    act_delta = dot(buffer[...], down_buffer[pl.ds(pl.multiple_of(step * rows, rows), rows)], (1, 1))
    pre_delta = (act_delta * slope[...].astype(F32)).astype(BF16)
    out[...] = pre_delta
    sums[places[step]] = jnp.sum(pre_delta.astype(F32), axis=0, keepdims=True)


def hidden_back(blocks, downs, slope, places):
    tokens, width = blocks[0].shape
    length, count, rows = tokens * len(blocks), len(downs), downs[0].shape[0]
    return pl.pallas_call(
        functools.partial(hidden_back_kernel, count, len(blocks)),
        grid_spec=pltpu.PrefetchScalarGridSpec(
            num_scalar_prefetch=1,
            grid=(count,),
            in_specs=[pl.BlockSpec((length, rows), lambda step, _: (0, step))]
            + [ANYWHERE] * (count + len(blocks)),
            out_specs=[
                pl.BlockSpec((length, rows), lambda step, _: (0, step)),
                pl.BlockSpec((count, 1, rows), lambda step, _: (0, 0, 0)),
            ],
            scratch_shapes=[
                pltpu.VMEM((length, width), BF16),
                pltpu.VMEM((count * rows, width), BF16),
                pltpu.SemaphoreType.DMA((len(blocks),)),
                pltpu.SemaphoreType.DMA((count,)),
            ],
        ),
        out_shape=[
            jax.ShapeDtypeStruct((length, count * rows), BF16),
            jax.ShapeDtypeStruct((count, 1, rows), F32),
        ],
        name="hidden_back",
        cost_estimate=cost(2 * length * width * count * rows, 2 * length * (width + 2 * count * rows)),
    )(places, slope, *downs, *blocks)


def unit_back_kernel(count, picked, places, gain_one, gain_two, pre_delta, joined_delta, *refs):
    blocks, refs = refs[: len(picked)], refs[len(picked) :]
    ups, ins, refs = refs[:count], refs[count : 2 * count], refs[2 * count :]
    outs, refs = refs[:-12], refs[-12:]
    (sums, pre_buffer, joined_buffer, block_buffer, up_buffer, in_buffer, unit, pre_sems, block_sems,
     joined_sems, up_sems, in_sems) = refs
    share, columns = outs[0].shape
    tokens = blocks[0].shape[0]
    head_width = joined_delta.shape[2]
    steps = up_buffer.shape[1] // columns
    block_moves = copies(blocks, row_targets(block_buffer, blocks), block_sems)
    joined_moves = copies(
        [joined_delta.at[part, index * tokens : (index + 1) * tokens] for part in range(3) for index in picked],
        [
            target.at[:, part * head_width : (part + 1) * head_width]
            for part in range(3)
            for target in row_targets(joined_buffer, blocks)
        ],
        joined_sems,
    )
    pre_moves = copies(
        [pre_delta.at[index * tokens : (index + 1) * tokens] for index in picked],
        row_targets(pre_buffer, blocks),
        pre_sems,
    )
    paired = count == steps
    in_moves = [
        pltpu.make_async_copy(piece, target, in_sems.at[places[index] if paired else index])
        for index, (piece, target) in enumerate(zip(ins, row_targets(in_buffer, ins, places)))
    ]
    start_all(block_moves)
    up_moves = []
    for step in range(steps):
        place = slice(step * columns, (step + 1) * columns)
        up_moves.append(copies(
            [up.at[:, place] for up in ups],
            [target.at[:, place] for target in row_targets(up_buffer, ups)],
            up_sems.at[step],
        ))
        start_all(up_moves[-1])
        if step == 0:
            start_all(pre_moves + joined_moves + in_moves)
    wait_all(block_moves)

    @pl.when(pl.program_id(0) == 0)
    def _():
        unit[...] = normed(block_buffer[...].astype(F32))[0]

    for step in range(steps):
        wait_all(up_moves[step], step)
    wait_all(pre_moves)
    wait_all(joined_moves if paired else joined_moves + in_moves)
    at = pl.ds(pl.multiple_of(pl.program_id(0) * columns, columns), columns)
    if paired:
        pltpu.make_async_copy(ins[0], in_buffer.at[at], in_sems.at[pl.program_id(0)]).wait()
    second = dot(pre_buffer[...], up_buffer[:, at], (1, 0))
    first = dot(joined_buffer[...], in_buffer[at], (1, 1))
    total = (first * gain_one[...] + second * gain_two[...]).astype(BF16)
    for index, out in enumerate(outs):
        out[...] = total[index * share : (index + 1) * share]
    own = unit[:, at]
    for index, member in enumerate((first * own, first, second * own, second)):
        sums[index : index + 1] = jnp.sum(member, axis=0, keepdims=True)


def unit_back(blocks, picked, pre_delta, joined_delta, ups, ins, gain_one, gain_two, places, share=1):
    tokens, width = blocks[0].shape
    count, hidden, joined_width = len(ups), pre_delta.shape[1], 3 * joined_delta.shape[2]
    length, columns = tokens * len(picked), min(256, width)
    gain_spec = pl.BlockSpec((1, columns), lambda step, _: (0, step))
    return pl.pallas_call(
        functools.partial(unit_back_kernel, count, tuple(picked)),
        grid_spec=pltpu.PrefetchScalarGridSpec(
            num_scalar_prefetch=1,
            grid=(width // columns,),
            in_specs=[gain_spec] * 2 + [ANYWHERE] * (2 + len(picked) + 2 * count),
            out_specs=[pl.BlockSpec((tokens // share, columns), lambda step, _: (0, step))]
            * (share * len(picked))
            + [pl.BlockSpec((8, columns), lambda step, _: (0, step))],
            scratch_shapes=[
                pltpu.VMEM((length, hidden), BF16),
                pltpu.VMEM((length, joined_width), BF16),
                pltpu.VMEM((length, width), BF16),
                pltpu.VMEM((hidden, width), BF16),
                pltpu.VMEM((width, joined_width), BF16),
                pltpu.VMEM((length, width), F32),
                pltpu.SemaphoreType.DMA((len(picked),)),
                pltpu.SemaphoreType.DMA((len(picked),)),
                pltpu.SemaphoreType.DMA((3 * len(picked),)),
                pltpu.SemaphoreType.DMA((width // columns, count)),
                pltpu.SemaphoreType.DMA((count,)),
            ],
        ),
        out_shape=[jax.ShapeDtypeStruct((tokens // share, width), BF16)] * (share * len(picked))
        + [jax.ShapeDtypeStruct((8, width), F32)],
        name="unit_back",
        cost_estimate=cost(
            2 * length * width * (hidden + joined_width), 2 * (length + width) * (hidden + joined_width)
        ),
    )(
        places, gain_one, gain_two, pre_delta, joined_delta, *[blocks[index] for index in picked], *ups, *ins
    )


def norm_back_kernel(count, block, delta, *refs):
    mine, moved, out = refs[:count], refs[count:-1], refs[-1]
    unit, scale = normed(block[...].astype(F32))
    for share in range(count):

        @pl.when(pl.program_id(0) // (pl.num_programs(0) // count) == share)
        def _(share=share):
            unit_delta = mine[share][...].astype(F32) + moved[share][...].astype(F32)
            mean = jnp.mean(unit_delta, axis=-1, keepdims=True)
            along = jnp.mean(unit_delta * unit, axis=-1, keepdims=True)
            out[...] = delta[...].astype(F32) + scale * (unit_delta - mean - unit * along)


def norm_back(block, mine, moved, delta):
    tokens, width = block.shape
    count = len(mine)
    steps = 4 // count
    spec = pl.BlockSpec((tokens // 4, width), lambda step: (step, 0))
    shares = [
        pl.BlockSpec(
            (tokens // 4, width), lambda step, share=share: (jnp.clip(step - share * steps, 0, steps - 1), 0)
        )
        for share in range(count)
    ]
    return pl.pallas_call(
        functools.partial(norm_back_kernel, count),
        grid=(4,),
        in_specs=[spec] * 2 + shares * 2,
        out_specs=spec,
        out_shape=jax.ShapeDtypeStruct((tokens, width), F32),
        name="norm_back",
        cost_estimate=cost(20 * tokens * width, 12 * tokens * width),
    )(block, delta, *mine, *moved)


def normed(values):
    centred = values - jnp.mean(values, axis=-1, keepdims=True)
    scale = lax.rsqrt(jnp.mean(centred * centred, axis=-1, keepdims=True) + EPSILON)
    return centred * scale, scale


def gelu_pair(values):
    cumulative = 0.5 * (1.0 + lax.erf(values * 0.5**0.5))
    density = jnp.exp(-0.5 * values * values) * (0.5 / jnp.pi) ** 0.5
    return values * cumulative, cumulative + values * density


def local(
    hidden_in,
    lengths,
    cotangent,
    in_weight,
    in_bias,
    out_weight,
    out_bias,
    up_weight,
    up_bias,
    down_weight,
    down_bias,
    first_gain,
    first_shift,
    second_gain,
    second_shift,
):
    tokens, width = hidden_in.shape[1:]
    fsdp_count, seq_count = lax.axis_size("fsdp"), lax.axis_size("seq")
    fsdp_place, seq_place = lax.axis_index("fsdp"), lax.axis_index("seq")
    length = tokens * seq_count
    heads = HEADS // seq_count
    head_width = heads * HEAD_DIM
    hidden = up_weight.shape[0] * fsdp_count

    own = hidden_in.reshape(tokens, width)
    positions = seq_place * tokens + jnp.arange(tokens, dtype=jnp.int32)
    keep = (positions < lengths[0])[:, None]
    delta_own = jnp.where(keep, cotangent.reshape(tokens, width), jnp.zeros((), BF16))

    small = [in_bias, up_bias, out_bias, down_bias, first_gain, first_shift, second_gain, second_shift]
    sizes = [member.shape[0] for member in small]
    rows = in_weight.shape[0]
    total = fsdp_count * seq_count
    tables = rotary_tables(length)
    where = jnp.stack([lengths[0], seq_place.astype(jnp.int32)])
    paced = fsdp_count == 8 and seq_count == 4
    shuffle = [(i, (i % fsdp_count) * seq_count + i // fsdp_count) for i in range(total)]
    if paced:
        shuffle = [
            (f * 4 + z, (f ^ 4) * 4 + (z ^ 1) if (f < 4) == (z % 2 == 1) else f * 4 + z)
            for f in range(8)
            for z in range(4)
        ]

    def split_heads(columns):
        if not paced:
            return columns.reshape(-1, 3, seq_count, head_width).transpose(2, 0, 1, 3)
        columns = columns.reshape(-1, 3, 2, 4, 2, HEAD_DIM).transpose(4, 2, 0, 1, 3, 5)
        return columns.reshape(4, -1, 3, head_width)

    def join_heads(split):
        if not paced:
            return split.transpose(1, 2, 0, 3)
        split = split.reshape(2, 2, -1, 3, 4, HEAD_DIM).transpose(2, 3, 1, 4, 0, 5)
        return split.reshape(-1, 3, HEADS, HEAD_DIM)

    by_heads = split_heads(in_weight).reshape(seq_count * rows, 3 * head_width)

    def unpack(everywhere):
        picked = [everywhere[:, :, row, :size] for row, size in enumerate(sizes)]
        in_offset, up_offset = picked[:2]
        up_offset = lax.dynamic_index_in_dim(up_offset, seq_place, 1, keepdims=False)
        in_offset = split_heads(in_offset.reshape(1, 3, -1)).reshape(seq_count, 3 * head_width)
        in_offset = lax.dynamic_index_in_dim(in_offset, seq_place, 0)
        return (in_offset, up_offset[:, None]) + tuple(row.reshape(1, -1) for row in picked[2:])

    bias_sum = jnp.sum(delta_own.astype(F32), axis=0)

    def sums_by_place(joined_delta, norm_sums, up_sum):
        in_sum = jnp.sum(joined_delta.astype(F32), axis=1).reshape(1, 1, 3, head_width)
        in_sum = lax.dynamic_update_slice_in_dim(
            jnp.zeros((seq_count, 1, 3, head_width), F32), in_sum, seq_place, 0
        )
        sums = [join_heads(in_sum), bias_sum] + [norm_sums[index] for index in range(4)]
        sums = [member.reshape(fsdp_count, seq_count, -1) for member in sums]
        sums = jnp.concatenate(sums, axis=2).transpose(1, 0, 2)
        return sums.reshape(seq_count, -1), up_sum.reshape(fsdp_count, -1)

    def over_seq(got, rows):
        sums = jnp.sum(got, axis=0).reshape(fsdp_count, -1)
        return jnp.concatenate([sums, rows], axis=1)

    def owned_columns(in_back):
        split = in_back[0].reshape(seq_count, rows, 3, head_width)
        return join_heads(split).reshape(rows, -1).astype(F32)

    if paced:
        place_list = piece_places()
        first_mask, second_mask = cross_masks(jnp.arange(1, dtype=jnp.int32) * 0 + fsdp_place)
        kinds = jnp.arange(8, dtype=jnp.int32)
        masks = jnp.where((kinds & 1) == 1, second_mask, 0) ^ jnp.where((kinds & 2) == 2, first_mask, 0)
        pair_masks = jnp.where((kinds & 1) == 1, first_mask, 0) ^ jnp.where((kinds & 2) == 2, second_mask, 0)
        places = fsdp_place ^ jnp.where(kinds < 4, masks, 1 ^ pair_masks)
        out_places = (places & 3) * 2 + (places >> 2)
        out_where = jnp.concatenate([where, out_places])
        everywhere = small_everywhere(small_over(small))
        everywhere, own_first, up_first, out_weight, by_heads = together(
            everywhere, own, up_weight, out_weight, by_heads
        )
        block_1 = shift_seq(own_first, 1)
        up_2, up_1 = cross_second(up_first), cross_first(up_first)
        in_offset, up_offset, out_offset, down_offset, *scales = unpack(everywhere)
        both = norm_both(own, 0, seq_count, scales, [])
        block_1, up_2, up_1, first_in, second_in, by_heads = together(
            block_1, up_2, up_1, *both, by_heads
        )
        in_0 = exchange_seq(by_heads)
        up_3 = cross_first(up_2)
        mine = lax.ppermute(out_weight, AXES, shuffle)
        both = norm_both(block_1, 1, seq_count, scales, [first_in, second_in])
        ups = [up_first, up_2, up_1, up_3]
        mine, first_in, second_in, block_1, down_weight, in_0, *ups = together(
            mine, *both, block_1, down_weight, in_0, *ups
        )
        block_2 = shift_seq(block_1, 1)
        down_2, down_1 = cross_second(down_weight), cross_first(down_weight)
        ups_pair = [flip_fsdp(piece, 1) for piece in ups]
        in_0, block_2, down_2, down_1, first_in, second_in, *ups_pair = together(
            in_0, block_2, down_2, down_1, first_in, second_in, *ups_pair
        )
        ups = ups + ups_pair
        block_3 = shift_seq(block_2, 1)
        in_2, in_1 = cross_second(in_0), cross_first(in_0)
        out_2, out_1 = cross_second(mine), cross_first(mine)
        both = norm_both(block_2, 2, seq_count, scales, [first_in, second_in])
        block_3, in_2, in_1, out_2, out_1, down_2, first_in, second_in, delta_own = together(
            block_3, in_2, in_1, out_2, out_1, down_2, *both, delta_own
        )
        blocks = [own, block_1, block_2, block_3]
        delta_1 = shift_seq(delta_own, 1)
        in_3, down_3, out_3 = cross_first(in_2), cross_first(down_2), cross_first(out_2)
        ins = [in_0, in_2, in_1, in_3]
        ins = ins + [flip_fsdp(piece, 1) for piece in ins]
        first_in, second_in = norm_both(block_3, 3, seq_count, scales, [first_in, second_in])
        act, slope = hidden_forward(second_in, up_offset, ups, places)
        outs = [mine, out_2, out_1, out_3]
        delta_1, first_in, act, slope, down_3, *landed = together(
            delta_1, first_in, act, slope, down_3, *outs, *ins
        )
        outs, ins = landed[:4], landed[4:]
        delta_2 = shift_seq(delta_1, 1)
        downs = [down_weight, down_2, down_1, down_3]
        downs = downs + [flip_fsdp(piece, 1) for piece in downs]
        joined = project(first_in, ins, in_offset, places, 3)
        query, key_rows, value_rows, mixed = attend(joined, tables, where, heads, tokens)
        delta_2, mixed, act, *landed = together(delta_2, mixed, act, *outs, *downs)
        outs, downs = landed[:4], landed[4:]
        delta_3 = shift_seq(delta_2, 1)
        outs = outs + [flip_fsdp(piece, 1) for piece in outs]
        branches = branch_forward(mixed, outs, act, downs, out_places, 4)
        delta_3, act, *branches = together(delta_3, act, *branches)
        deltas = [delta_own, delta_1, delta_2, delta_3]

        same_pieces = jnp.arange(4, dtype=jnp.int32)
        other_pieces = same_pieces + 4
        piece = hidden // 8
        moving = shift_seq(branches[1], 1)
        joined_delta = attend_back(
            query, key_rows, value_rows, deltas, outs, tables, out_where, heads
        )
        joined_delta, mixed, moving, first_in = together(joined_delta, mixed, moving, first_in)
        in_other = outer(first_in, [joined_delta], width // 8, places[4:])
        in_other, first_in, joined_delta = together(in_other, first_in, joined_delta)
        in_given = flip_fsdp(in_other, 1)
        in_same = outer(first_in, [joined_delta], width // 8, places[:4])
        in_given, in_same, act = together(in_given, in_same, act)
        in_far, act = together(far_share(in_same, in_given), act)
        in_far = cross_first(in_far)
        down_other = outer(act, deltas, piece, other_pieces)
        in_far, down_other, act = together(in_far, down_other, act)
        in_near = near_shares(in_same, in_given, in_far)
        moving = joined_by(moving, branches[2])
        down_other, act, mixed, moving, *in_near = together(
            down_other, act, mixed, moving, *in_near
        )
        moving = shift_seq(moving, 1)
        in_near = send_near(*in_near)
        down_given = flip_fsdp(down_other, 1)
        down_same = outer(act, deltas, piece, same_pieces)
        out_delta = outer(mixed, deltas, head_width // 2, jnp.arange(2, dtype=jnp.int32))
        down_same, out_delta, down_given, slope, moving, *in_near = together(
            down_same, out_delta, down_given, slope, moving, *in_near
        )
        out_delta = out_delta.reshape(8, -1, width)
        out_delta = [pick(out_delta, (place & 3) * 2 + (place >> 2)) for place in place_list]
        out_same = jnp.concatenate(out_delta[:4], axis=0)
        out_other = jnp.concatenate(out_delta[4:], axis=0)
        down_far = far_share(down_same, down_given)
        in_rows = sum_near(in_same, in_given, *in_near).astype(BF16)
        down_far, out_other, slope, in_rows = together(down_far, out_other, slope, in_rows)
        down_far = cross_first(down_far)
        out_given = flip_fsdp(out_other, 1)
        in_back = [exchange_seq(in_rows)]
        pre_delta, up_sum = hidden_back(deltas, downs, slope, places)
        down_far, out_given, pre_delta, moving, *in_back = together(
            down_far, out_given, pre_delta, moving, *in_back
        )
        down_near = near_shares(down_same, down_given, down_far)
        out_far = far_share(out_same, out_given)
        moving = joined_by(moving, branches[3])
        out_far, pre_delta, moving, *down_near = together(out_far, pre_delta, moving, *down_near)
        summed = shift_seq(moving, 1)
        down_near = send_near(*down_near)
        out_far = cross_first(out_far)
        *units, sums_early = unit_back(
            blocks, (1, 2), pre_delta, joined_delta, ups, ins, scales[0], scales[2], places, share=2
        )
        pre_delta, out_far, sums_early, summed, *landed = together(
            pre_delta, out_far, sums_early, summed, *units, *down_near, *in_back
        )
        units, down_near, in_back = landed[:4], landed[4:6], landed[6:]
        out_near = near_shares(out_same, out_given, out_far)
        pre_delta, *landed = together(pre_delta, *units, *out_near)
        units, out_near = landed[:4], landed[4:]
        unit_halves = [shift_seq(units[0], 1), units[1]]
        out_near = send_near(*out_near)
        up_other = outer(pre_delta, [second_in], piece, other_pieces)
        up_other, pre_delta, second_in, *landed = together(
            up_other, pre_delta, second_in, *unit_halves, *out_near, *in_back, *down_near
        )
        unit_halves, out_near, in_back, down_near = landed[:2], landed[2:4], landed[4:5], landed[5:]
        unit_halves[1] = shift_seq(unit_halves[1], 1)
        up_given = flip_fsdp(up_other, 1)
        up_same = outer(pre_delta, [second_in], piece, same_pieces)
        up_same, up_given, pre_delta, *landed = together(
            up_same, up_given, pre_delta, *unit_halves, *in_back, *out_near, *down_near
        )
        unit_halves, in_back, out_near, down_near = landed[:2], landed[2:3], landed[3:5], landed[5:]
        unit_moving = joined_by(jnp.concatenate(unit_halves, axis=0), jnp.concatenate(units[2:], axis=0))
        up_far = far_share(up_same, up_given)
        out_mine = sum_near(out_same, out_given, *out_near)
        unit_moving, up_far, out_mine, pre_delta = together(unit_moving, up_far, out_mine, pre_delta)
        unit_moving = shift_seq(unit_moving, 1)
        up_far = cross_first(up_far)
        out_gradient = lax.ppermute(out_mine, AXES, [(target, origin) for origin, target in shuffle])
        unit_last, unit_own, sums_late = unit_back(
            blocks, (3, 0), pre_delta, joined_delta, ups, ins, scales[0], scales[2], places
        )
        out_gradient, unit_moving, up_far, unit_last, unit_own, sums_late, *landed = together(
            out_gradient, unit_moving, up_far, unit_last, unit_own, sums_late, *in_back, *down_near
        )
        in_back, down_near = landed[:1], landed[1:]
        sums, rows_sum = sums_by_place(joined_delta, sums_early + sums_late, up_sum)
        unit_moving = joined_by(unit_moving, unit_last)
        up_near = near_shares(up_same, up_given, up_far)
        unit_moving, sums, *up_near = together(unit_moving, sums, *up_near)
        unit_moving = shift_seq(unit_moving, 1)
        up_near = send_near(*up_near)
        sums = small_exchange(sums, "seq")
        in_gradient = owned_columns(in_back)
        down_gradient = sum_near(down_same, down_given, *down_near)
        unit_moving, down_gradient, in_gradient, sums, *up_near = together(
            unit_moving, down_gradient, in_gradient, sums, *up_near
        )
        small_result = jnp.sum(small_exchange(over_seq(sums, rows_sum), "fsdp"), axis=0)
        up_gradient = sum_near(up_same, up_given, *up_near)
        summed = branches[0].astype(F32) + summed.astype(F32)
        input_gradient = norm_back(own, [unit_own], [unit_moving], delta_own)
    else:
        in_offset, up_offset, out_offset, down_offset, *scales = unpack(small_everywhere(small_over(small)))
        by_heads = exchange_seq(by_heads)
        mine = lax.ppermute(out_weight, AXES, shuffle)
        ups, downs, ins, outs = (
            [lax.all_gather(member, "fsdp", axis=0, tiled=True)]
            for member in (up_weight, down_weight, by_heads, mine)
        )
        places = jnp.zeros((1,), jnp.int32)
        up_offset = up_offset.reshape(1, 1, -1)
        blocks, deltas = [own], [delta_own]
        for _ in range(seq_count - 1):
            blocks.append(shift_seq(blocks[-1], 1))
            deltas.append(shift_seq(deltas[-1], 1))
        both = []
        for index, block in enumerate(blocks):
            both = norm_both(block, index, seq_count, scales, both)
        first_in, second_in = both
        act, slope = hidden_forward(second_in, up_offset, ups, places)
        joined = project(first_in, ins, in_offset, places, 3)
        query, key_rows, value_rows, mixed = attend(joined, tables, where, heads, tokens)
        branches = branch_forward(mixed, outs, act, downs, places, seq_count)
        quarters = jnp.arange(4, dtype=jnp.int32)
        down_gradient = scatter_whole(outer(act, deltas, hidden // 4, quarters))
        joined_delta = attend_back(
            query, key_rows, value_rows, deltas, outs, tables, jnp.concatenate([where, places]), heads
        )
        pre_delta, up_sum = hidden_back(deltas, downs, slope, places)
        in_rows = scatter_whole(outer(first_in, [joined_delta], width // 4, quarters))
        in_back = [exchange_seq(in_rows.astype(BF16).reshape(seq_count * rows, 3 * head_width))]
        *units, norm_sums = unit_back(
            blocks, range(seq_count), pre_delta, joined_delta, ups, ins, scales[0], scales[2], places
        )
        up_gradient = scatter_whole(outer(pre_delta, [second_in], hidden // 4, quarters))
        out_mine = scatter_whole(outer(mixed, deltas, head_width // 2, quarters[:2]))
        summed, unit_moving = shift_seq(branches[1], 1), shift_seq(units[1], 1)
        for index in range(2, seq_count):
            summed = shift_seq(joined_by(summed, branches[index]), 1)
            unit_moving = shift_seq(joined_by(unit_moving, units[index]), 1)
        out_gradient = lax.ppermute(out_mine, AXES, [(target, origin) for origin, target in shuffle])
        in_gradient = owned_columns(in_back)
        sums, rows_sum = sums_by_place(joined_delta, norm_sums, up_sum)
        sums = over_seq(small_exchange(sums, "seq"), rows_sum)
        small_result = jnp.sum(small_exchange(sums, "fsdp"), axis=0)
        summed = branches[0].astype(F32) + summed.astype(F32)
        input_gradient = norm_back(own, [units[0]], [unit_moving], delta_own)

    source = own.astype(F32)
    layer_output = jnp.where(keep, source + summed + (out_offset + down_offset), 0.0)
    at, pieces = 0, []
    for size in (sizes[0],) + (sizes[2],) * 5 + (sizes[1],):
        pieces.append(small_result[at : at + size])
        at += size
    in_bias_gradient, bias_gradient, gain_one_g, shift_one_g, gain_two_g, shift_two_g, up_bias_g = pieces
    return (
        layer_output[None],
        input_gradient[None],
        in_gradient,
        in_bias_gradient,
        out_gradient,
        bias_gradient,
        up_gradient,
        up_bias_g,
        down_gradient,
        bias_gradient,
        gain_one_g,
        shift_one_g,
        gain_two_g,
        shift_two_g,
    )


def solution(mesh):
    tokens, matrix, vector = P("fsdp", "seq", None), P(AXES, None), P(AXES)
    return jax.shard_map(
        local,
        mesh=mesh,
        in_specs=(tokens, P("fsdp"), tokens, matrix, vector, matrix, vector, matrix, vector, matrix)
        + (vector,) * 5,
        out_specs=(tokens, tokens, matrix, vector, matrix, vector, matrix, vector, matrix)
        + (vector,) * 5,
        check_vma=False,
    )
```
